32 devices in a mesh: dom: 8 (over z, y), rep: 4 (over x, core).
Axes of the slice: x: 2, y: 2, z: 4, core: 2. Of those that a mesh axis runs over, the one named last changes fastest.
Arguments:
- embedding: float32 [4096, 400], P('dom'), may hold values from -1.5 to 1.5
- adagrad_sum: float32 [4096], P('dom'), may hold values from 0.01 to 1
- row_lists: int32 [4, 8, 8, 16], P('rep', 'dom'), may hold values from 0 to 511, as said below
- source_slots: int32 [4, 8, 2, 512], P('rep', 'dom'), may hold values from 0 to 127, as said below
- target_slots: int32 [4, 8, 2, 512], P('rep', 'dom'), may hold values from 0 to 127, as said below
- negative_ids: int32 [4, 8, 2, 2, 512], P('rep', 'dom'), may hold values from 0 to 511
Outputs:
- new_embedding: float32 [4096, 400], P('dom')
- new_adagrad_sum: float32 [4096], P('dom')
The draws below stay inside these ranges and needn't reach their ends.
Inputs may be any that keep to these rules, and one draw needn't show every extreme that they name: `row_lists`: for each worker and owner, a count of leading entries are distinct rows of that owner and the other entries are 0. For the worker with index w along dom, the owners (w + c) mod 8, c < 4, have all 16 entries live; every other owner has 1 to 8 live entries. `source_slots`: every slot named is among the leading live entries of the worker's row list for its owner; entries k >= 8 are named only for the owners (w + c) mod 8, c < 4, of the worker with index w along dom. `target_slots`: every slot named is among the leading live entries of the worker's row list for its owner; entries k >= 8 are named only for the owners (w + c) mod 8, c < 4, of the worker with index w along dom.
All inputs are finite; a program needn't handle non-finite values.
Results may differ from the reference program's by a relative error of at most 0.0003.
Values sent between devices are 32-bit elements; how exact they have to be, the bound alone decides.
A program may use at most 64 MiB of HBM per device.

```python
import math
import jax
import jax.numpy as jnp
from jax import lax

D = 400
ROWS_DEV = 512
EDGES = 512
NEGS = 512
BATCHES = 2
SLOTS = 16
HEAVY = 4
OWNERS = 8
GROUPS = 4
NODES = 4096


def plan_counts(key):
    base_key = jax.random.fold_in(key, 11)
    lowest = max(SLOTS // 4, 1)
    others = jax.random.randint(jax.random.fold_in(base_key, 3), (GROUPS, OWNERS, OWNERS), lowest, SLOTS // 2 + 1)
    workers = jnp.arange(OWNERS, dtype=jnp.int32)[:, None]
    owners = jnp.arange(OWNERS, dtype=jnp.int32)[None, :]
    heavy = (owners - workers) % OWNERS < HEAVY
    return jnp.where(heavy[None], SLOTS, others).astype(jnp.int32)


def edge_slots(key, which):
    counts = plan_counts(key)
    edge_key = jax.random.fold_in(key, 20 + which)
    shape = (GROUPS, OWNERS, BATCHES * EDGES)
    picks = jax.random.randint(jax.random.fold_in(edge_key, 1), shape, 0, OWNERS * SLOTS)
    owner = picks // SLOTS
    within = picks % SLOTS
    live = jnp.take_along_axis(counts, owner, axis=2)
    spread = owner * SLOTS + within % live
    workers = jnp.arange(OWNERS, dtype=jnp.int32)[None, :, None]
    reach = jax.random.randint(jax.random.fold_in(edge_key, 2), shape, 0, HEAVY)
    place = jax.random.randint(jax.random.fold_in(edge_key, 3), shape, 0, SLOTS)
    focused = (workers + reach) % OWNERS * SLOTS + place
    coin = jax.random.randint(jax.random.fold_in(edge_key, 4), shape, 0, 2)
    slots = jnp.where(coin == 0, focused, spread)
    return slots.reshape(GROUPS, OWNERS, BATCHES, EDGES).astype(jnp.int32)


def draw_row_lists(key, part):
    counts = plan_counts(key)
    list_key = jax.random.fold_in(key, 12)
    starts = jax.random.randint(jax.random.fold_in(list_key, 1), (GROUPS, OWNERS, OWNERS, 1), 0, ROWS_DEV)
    strides = 2 * jax.random.randint(jax.random.fold_in(list_key, 2), (GROUPS, OWNERS, OWNERS, 1), 0, ROWS_DEV // 2) + 1
    places = jnp.arange(SLOTS, dtype=jnp.int32)
    rows = (starts + places * strides) % ROWS_DEV
    return jnp.where(places < counts[..., None], rows, 0).astype(jnp.int32)


def draw_source_slots(key, part):
    return edge_slots(key, 0)


def draw_target_slots(key, part):
    return edge_slots(key, 1)


def with_ends(drawn, key, least, top_value):
    dims = drawn.shape
    spot = [jax.random.randint(jax.random.fold_in(key, axis), (), 0, dims[axis]) for axis in range(len(dims))]
    drawn = drawn.at[tuple(spot)].set(least)
    longest = dims.index(max(dims))
    spot[longest] = (spot[longest] + 1) % dims[longest]
    return drawn.at[tuple(spot)].set(top_value)


def shard_levels(stream_key, dims, shards, smallest, top_value):
    level = 1.0
    for axis_at, blocks in shards:
        steps = jax.random.uniform(jax.random.fold_in(jax.random.fold_in(stream_key, 6), axis_at), (blocks,), jnp.float32, smallest / len(shards), top_value / len(shards))
        level = level * jnp.repeat(jnp.exp(steps), dims[axis_at] // blocks).reshape((-1,) + (1,) * (len(dims) - 1 - axis_at))
    return level


def scatter_about(own_key, shape, width, most, shards=(), kind=jnp.bfloat16):
    factor_of = shard_levels(own_key, shape, shards, -0.22, 0.18) if shards else 1.0
    array = jax.random.normal(own_key, shape, jnp.float32) * width * factor_of
    return jnp.minimum(jnp.maximum(array, -most), most).astype(kind)


def setup_inputs(seed: int = 0) -> dict:
    streams_of = jax.random.split(jax.random.key(seed), 7)
    return {
        "embedding": scatter_about(streams_of[0], (NODES, D), 0.25, 1.5, ((0, 8),), jnp.float32),
        "adagrad_sum": jnp.clip(jnp.exp(math.log(1.0) - 4.6051702 * jax.random.uniform(streams_of[1], (NODES,), jnp.float32) ** shard_levels(streams_of[1], (NODES,), ((0, 8),), -0.2, 0.2)), 0.01, 1.0),
        "row_lists": draw_row_lists(jax.random.fold_in(streams_of[6], 71), 0),
        "source_slots": draw_source_slots(jax.random.fold_in(streams_of[6], 71), 0),
        "target_slots": draw_target_slots(jax.random.fold_in(streams_of[6], 71), 0),
        "negative_ids": with_ends(jax.random.randint(streams_of[5], (GROUPS, OWNERS, BATCHES, 2, NEGS), 0, EDGES), jax.random.fold_in(streams_of[5], 1), 0, EDGES - 1).astype(jnp.int32),
    }


learn_rate = 0.1

def batch_grads(buffer, sources, targets, neg_dst, neg_src):
    highest = lax.Precision.HIGHEST
    src_rows = buffer[sources]
    dst_rows = buffer[targets]
    neg_dst_rows = buffer[targets[neg_dst]]
    neg_src_rows = buffer[sources[neg_src]]
    samples = neg_dst.shape[0]
    positive = lax.optimization_barrier(jnp.sum(src_rows * dst_rows, axis=1))
    pos_weight = -jax.nn.sigmoid(-positive)[:, None]
    dst_scores = jnp.dot(src_rows, neg_dst_rows.T, precision=highest)
    src_scores = jnp.dot(dst_rows, neg_src_rows.T, precision=highest)
    dst_weight = jax.nn.sigmoid(dst_scores) / samples
    src_weight = jax.nn.sigmoid(src_scores) / samples
    grad_src = pos_weight * dst_rows + jnp.dot(dst_weight, neg_dst_rows, precision=highest)
    grad_dst = pos_weight * src_rows + jnp.dot(src_weight, neg_src_rows, precision=highest)
    grad_negd = jnp.dot(dst_weight.T, src_rows, precision=highest)
    grad_negs = jnp.dot(src_weight.T, dst_rows, precision=highest)
    gradient = jnp.zeros(buffer.shape, buffer.dtype)
    gradient = gradient.at[sources].add(grad_src).at[targets].add(grad_dst)
    gradient = gradient.at[targets[neg_dst]].add(grad_negd).at[sources[neg_src]].add(grad_negs)
    return gradient

def reference(embedding, adagrad_sum, row_lists, source_slots, target_slots, negative_ids):
    offsets = (jnp.arange(OWNERS, dtype=jnp.int32) * ROWS_DEV)[:, None]
    lists = row_lists.reshape(GROUPS * OWNERS, OWNERS, SLOTS)
    sources_all = source_slots.reshape(GROUPS * OWNERS, BATCHES, EDGES)
    targets_all = target_slots.reshape(GROUPS * OWNERS, BATCHES, EDGES)
    negatives = negative_ids.reshape(GROUPS * OWNERS, BATCHES, 2, NEGS)

    def worker(summed, inputs):
        request, sources, targets, negs = inputs
        global_rows = (request.astype(jnp.int32) + offsets).reshape(-1)
        buffer = embedding[global_rows]
        gradient = jnp.zeros(buffer.shape, buffer.dtype)
        for batch in range(BATCHES):
            gradient = gradient + batch_grads(buffer, sources[batch], targets[batch], negs[batch, 0], negs[batch, 1])
        return (summed.at[global_rows].add(gradient), None)
    row_grad, unused = lax.scan(worker, jnp.zeros(embedding.shape, embedding.dtype), (lists, sources_all, targets_all, negatives))
    new_sum = adagrad_sum + lax.optimization_barrier(jnp.mean(row_grad * row_grad, axis=1))
    new_rows = embedding - learn_rate * row_grad / jnp.sqrt(new_sum)[:, None]
    return (new_rows, new_sum)
```

```python
import jax
import jax.numpy as jnp
from jax import lax
from jax.sharding import PartitionSpec as P

learn_rate = 0.1
HI = lax.Precision.HIGHEST


def slot_gradient(buffer, sources, targets, negatives):
    slots = buffer.shape[0]
    samples = negatives.shape[2]
    edges = sources.shape[1]
    ids = jnp.arange(slots, dtype=jnp.int32)
    src_hot = (sources[:, :, None] == ids).astype(jnp.float32)
    dst_hot = (targets[:, :, None] == ids).astype(jnp.float32)
    times = jnp.sum((negatives[:, :, :, None] == jnp.arange(edges, dtype=jnp.int32)).astype(jnp.float32), axis=2)
    cs = jnp.sum(src_hot, axis=1)
    ct = jnp.sum(dst_hot, axis=1)
    cp = jnp.sum(times[:, 0, :, None] * dst_hot, axis=1)
    cq = jnp.sum(times[:, 1, :, None] * src_hot, axis=1)
    pairs = jnp.sum(cs[:, :, None] * cp[:, None, :] + ct[:, :, None] * cq[:, None, :], axis=0)
    flat = (-1, slots)
    counts = lax.dot_general(
        src_hot.reshape(flat).astype(jnp.bfloat16), dst_hot.reshape(flat).astype(jnp.bfloat16),
        (((0,), (0,)), ((), ())), preferred_element_type=jnp.float32,
    )
    gram = jnp.dot(buffer, buffer.T, precision=HI)
    mixed = pairs * (jax.nn.sigmoid(gram) / samples) - counts * jax.nn.sigmoid(-gram)
    return jnp.dot(mixed + mixed.T, buffer, precision=HI)


def adagrad(rows_now, sum_now, row_grad):
    new_sum = sum_now + jnp.mean(row_grad * row_grad, axis=1)
    new_rows = rows_now - learn_rate * row_grad / jnp.sqrt(new_sum)[:, None]
    return (new_rows, new_sum)


def local(embedding, adagrad_sum, row_lists, source_slots, target_slots, negative_ids):
    requests = row_lists[0, 0]
    owners, capacity = requests.shape
    rows, width = embedding.shape
    incoming = lax.all_to_all(requests, "dom", split_axis=0, concat_axis=0, tiled=True)
    wanted = (incoming.reshape(-1)[:, None] == jnp.arange(rows, dtype=jnp.int32)).astype(jnp.float32)
    picked = jnp.dot(wanted, embedding, precision=HI).reshape(owners, capacity, width)
    pulled = lax.all_to_all(picked, "dom", split_axis=0, concat_axis=0, tiled=True)
    buffer = pulled.reshape(owners * capacity, width)
    gradient = slot_gradient(buffer, source_slots[0, 0], target_slots[0, 0], negative_ids[0, 0])
    returned = lax.all_to_all(
        gradient.reshape(owners, capacity, width), "dom", split_axis=0, concat_axis=0, tiled=True
    )
    owned = lax.dot_general(wanted, returned.reshape(-1, width), (((0,), (0,)), ((), ())), precision=HI)
    summed = lax.psum(owned, "rep")
    return adagrad(embedding, adagrad_sum, summed)


def solution(mesh):
    in_specs = (
        P("dom", None),
        P("dom"),
        P("rep", "dom", None, None),
        P("rep", "dom", None, None),
        P("rep", "dom", None, None),
        P("rep", "dom", None, None, None),
    )
    out_specs = (P("dom", None), P("dom"))
    return jax.shard_map(local, mesh=mesh, in_specs=in_specs, out_specs=out_specs, check_vma=False)
```

```python
import functools
import jax
import jax.numpy as jnp
from jax import lax
from jax.experimental import pallas as pl
from jax.experimental.pallas import tpu as pltpu
from jax.sharding import PartitionSpec as P

learn_rate = 0.1
HI = lax.Precision.HIGHEST
HEAVY = 4
LIGHT_ROWS = 8
MESH = pl.DeviceIdType.MESH
BF = jnp.bfloat16
F32 = jnp.float32


def mm(a, b):
    return lax.dot_general(a, b, (((1,), (0,)), ((), ())), preferred_element_type=F32)


def mm_nt(a, b):
    return lax.dot_general(a, b, (((1,), (1,)), ((), ())), preferred_element_type=F32)


def parts_of(x, count):
    parts = []
    for _ in range(count):
        part = x.astype(BF)
        parts.append(part)
        x = x - part.astype(F32)
    return parts


def hot(mask):
    return mask.astype(F32).astype(BF)


def pair_counts(src_ref, dst_ref, neg_ref, slots):
    batches, edges = src_ref.shape[2:]
    samples = neg_ref.shape[4]
    slot_id = lax.broadcasted_iota(jnp.int32, (slots, edges), 0)
    edge_id = lax.broadcasted_iota(jnp.int32, (edges, samples), 0)
    ones = jnp.ones((8, samples), BF)
    pairs = jnp.zeros((slots, slots), F32)
    counts = jnp.zeros((slots, slots), F32)
    for b in range(batches):
        src_mask = (slot_id == src_ref[0, 0, b : b + 1, :]).astype(F32)
        dst_mask = (slot_id == dst_ref[0, 0, b : b + 1, :]).astype(F32)
        src_hot = src_mask.astype(BF)
        dst_hot = dst_mask.astype(BF)
        counts += mm_nt(src_hot, dst_hot)
        for side, (near, far) in enumerate(((src_mask, dst_hot), (dst_mask, src_hot))):
            chosen = hot(edge_id == neg_ref[0, 0, b, side : side + 1, :])
            negative = mm(far, chosen).astype(BF)
            times = mm_nt(ones, negative)[0:1, :]
            pairs += jnp.sum(near, axis=1, keepdims=True) * times
    return (pairs + pairs.T) * (1.0 / samples), counts + counts.T


def kernel(
    ndom, nrep,
    emb_ref, lists_ref, src_ref, dst_ref, neg_ref, out_ref,
    req_send, req_recv, pull_send, buf, grad_send, grad_recv, ids_all,
    req_ss, req_rs, pull_ss, pull_rs, ret_ss, ret_rs, rep_ss, rep_rs, ids_ss, ids_rs,
):
    me = lax.axis_index("dom")
    rep = lax.axis_index("rep")
    rows, width = emb_ref.shape
    capacity = lists_ref.shape[3]
    slots = ndom * capacity

    def up(c):
        return lax.rem(me + c, ndom)

    def down(c):
        return lax.rem(me + ndom - c, ndom)

    def rep_peer(k):
        return lax.rem(rep + k, nrep)

    def size(c):
        return capacity if c < HEAVY else min(LIGHT_ROWS, capacity)

    buf[...] = jnp.zeros_like(buf)
    grad_recv[...] = jnp.zeros_like(grad_recv)
    own_lists = lists_ref[0, 0]
    if slots > capacity:
        own_lists = jnp.concatenate([own_lists, jnp.zeros((ndom, slots - capacity), jnp.int32)], axis=1)
    own_lists = pltpu.roll(own_lists, me * capacity, 1)
    for o in range(ndom):
        req_send[o] = jnp.broadcast_to(own_lists[o : o + 1, :], (8, slots))

    barrier = pltpu.get_barrier_semaphore()
    for c in range(1, ndom):
        pl.semaphore_signal(barrier, inc=1, device_id={"dom": up(c)}, device_id_type=MESH)
    for k in range(1, nrep):
        pl.semaphore_signal(barrier, inc=1, device_id={"rep": rep_peer(k)}, device_id_type=MESH)
    pl.semaphore_wait(barrier, ndom - 1 + nrep - 1)

    def remote(src, dst, send, recv, target):
        return pltpu.make_async_remote_copy(
            src_ref=src, dst_ref=dst, send_sem=send, recv_sem=recv, device_id=target, device_id_type=MESH
        )

    asks = []
    for c in range(1, ndom):
        ask = remote(req_send.at[up(c)], req_recv.at[c], req_ss.at[c], req_rs.at[c], {"dom": up(c)})
        ask.start()
        asks.append(ask)

    pairs, counts = pair_counts(src_ref, dst_ref, neg_ref, slots)
    emb_parts = parts_of(emb_ref[...], 3)

    ids = req_send[me]
    for c in range(1, ndom):
        asks[c - 1].wait_recv()
        ids = ids + req_recv[c]
    ids_all[rep] = ids

    wanted = hot(lax.broadcasted_iota(jnp.int32, (slots, rows), 1) == ids.T[:, 0:1])
    pulled = mm(wanted, emb_parts[0]) + mm(wanted, emb_parts[1]) + mm(wanted, emb_parts[2])
    pull_send[...] = pulled.reshape(ndom, capacity, width)
    pulls = []
    for c in range(1, ndom):
        live = pl.ds(0, size(c))
        pull = remote(
            pull_send.at[down(c), live], buf.at[me, live], pull_ss.at[c], pull_rs.at[c], {"dom": down(c)}
        )
        pull.start()
        pulls.append(pull)
    buf[me] = pull_send[me]
    tells = []
    for k in range(1, nrep):
        tell = remote(ids_all.at[rep], ids_all.at[rep], ids_ss.at[k], ids_rs.at[k], {"rep": rep_peer(k)})
        tell.start()
        tells.append(tell)

    for c in range(1, ndom):
        live = pl.ds(0, size(c))
        remote(buf.at[up(c), live], buf.at[up(c), live], pull_ss.at[c], pull_rs.at[c], {"dom": up(c)}).wait_recv()
    buffer = buf[...].reshape(slots, width)
    gram = lax.dot_general(buffer, buffer, (((1,), (1,)), ((), ())), precision=HI, preferred_element_type=F32)
    mixed = pairs * jax.nn.sigmoid(gram) - counts * jax.nn.sigmoid(-gram)
    gradient = jnp.dot(mixed, buffer, precision=HI, preferred_element_type=F32)
    grad_send[...] = gradient.reshape(ndom, capacity, width)

    returns = []
    for c in range(1, ndom):
        live = pl.ds(0, size(c))
        back = remote(
            grad_send.at[up(c), live], grad_recv.at[rep, me, live], ret_ss.at[c], ret_rs.at[c], {"dom": up(c)}
        )
        back.start()
        returns.append(back)
    grad_recv[rep, me] = grad_send[me]

    shares = []
    for c in range(ndom):
        block = grad_recv.at[rep, down(c), pl.ds(0, size(c))]
        if c > 0:
            remote(block, block, ret_ss.at[c], ret_rs.at[c], {"dom": down(c)}).wait_recv()
        for k in range(1, nrep):
            share = remote(block, block, rep_ss.at[k, c], rep_rs.at[k, c], {"rep": rep_peer(k)})
            share.start()
            shares.append(share)

    for k in range(1, nrep):
        tells[k - 1].wait_recv()
        source = rep_peer(nrep - k)
        for c in range(ndom):
            block = grad_recv.at[source, down(c), pl.ds(0, size(c))]
            remote(block, block, rep_ss.at[k, c], rep_rs.at[k, c], {"rep": source}).wait_recv()

    row_id = lax.broadcasted_iota(jnp.int32, (rows, slots), 0)
    total = jnp.zeros((rows, width), F32)
    for g in range(nrep):
        owned = hot(row_id == ids_all[g, 0:1, :])
        for part in parts_of(grad_recv[g].reshape(slots, width), 2):
            total += mm(owned, part)
    out_ref[...] = total

    for copy in asks + pulls + tells + returns + shares:
        copy.wait_send()


def local(ndom, nrep, embedding, adagrad_sum, row_lists, source_slots, target_slots, negative_ids):
    rows, width = embedding.shape
    capacity = row_lists.shape[3]
    slots = ndom * capacity
    dma = pltpu.SemaphoreType.DMA
    vmem = pl.BlockSpec(memory_space=pltpu.VMEM)
    row_grad = pl.pallas_call(
        functools.partial(kernel, ndom, nrep),
        out_shape=jax.ShapeDtypeStruct((rows, width), F32),
        in_specs=[vmem] * 5,
        out_specs=vmem,
        scratch_shapes=[
            pltpu.VMEM((ndom, 8, slots), jnp.int32),
            pltpu.VMEM((ndom, 8, slots), jnp.int32),
            pltpu.VMEM((ndom, capacity, width), F32),
            pltpu.VMEM((ndom, capacity, width), F32),
            pltpu.VMEM((ndom, capacity, width), F32),
            pltpu.VMEM((nrep, ndom, capacity, width), F32),
            pltpu.VMEM((nrep, 8, slots), jnp.int32),
            dma((ndom,)), dma((ndom,)), dma((ndom,)), dma((ndom,)), dma((ndom,)), dma((ndom,)),
            dma((nrep, ndom)), dma((nrep, ndom)), dma((nrep,)), dma((nrep,)),
        ],
        compiler_params=pltpu.CompilerParams(
            collective_id=0, has_side_effects=True, vmem_limit_bytes=60 * 1024 * 1024
        ),
    )(embedding, row_lists, source_slots, target_slots, negative_ids)
    new_sum = adagrad_sum + jnp.mean(row_grad * row_grad, axis=1)
    new_rows = embedding - learn_rate * row_grad / jnp.sqrt(new_sum)[:, None]
    return (new_rows, new_sum)


def solution(mesh):
    in_specs = (
        P("dom", None),
        P("dom"),
        P("rep", "dom", None, None),
        P("rep", "dom", None, None),
        P("rep", "dom", None, None),
        P("rep", "dom", None, None, None),
    )
    out_specs = (P("dom", None), P("dom"))
    body = functools.partial(local, mesh.shape["dom"], mesh.shape["rep"])
    return jax.shard_map(body, mesh=mesh, in_specs=in_specs, out_specs=out_specs, check_vma=False)
```

```python
import functools
import jax
import jax.numpy as jnp
from jax import lax
from jax.experimental import pallas as pl
from jax.experimental.pallas import tpu as pltpu
from jax.sharding import PartitionSpec as P

learn_rate = 0.1
HI = lax.Precision.HIGHEST
HEAVY = 4
LIGHT_ROWS = 8
MESH = pl.DeviceIdType.MESH
BF = jnp.bfloat16
F32 = jnp.float32


def mm(a, b):
    return lax.dot_general(a, b, (((1,), (0,)), ((), ())), preferred_element_type=F32)


def mm_nt(a, b):
    return lax.dot_general(a, b, (((1,), (1,)), ((), ())), preferred_element_type=F32)


def parts_of(x, count):
    parts = []
    for _ in range(count):
        part = x.astype(BF)
        parts.append(part)
        x = x - part.astype(F32)
    return parts


def hot(mask):
    return mask.astype(F32).astype(BF)


def pair_counts(src_ref, dst_ref, neg_ref, slots):
    batches, edges = src_ref.shape[2:]
    samples = neg_ref.shape[4]
    slot_id = lax.broadcasted_iota(jnp.int32, (slots, edges), 0)
    edge_id = lax.broadcasted_iota(jnp.int32, (edges, samples), 0)
    ones = jnp.ones((8, samples), BF)
    pairs = jnp.zeros((slots, slots), F32)
    counts = jnp.zeros((slots, slots), F32)
    for b in range(batches):
        src_mask = (slot_id == src_ref[0, 0, b : b + 1, :]).astype(F32)
        dst_mask = (slot_id == dst_ref[0, 0, b : b + 1, :]).astype(F32)
        src_hot = src_mask.astype(BF)
        dst_hot = dst_mask.astype(BF)
        counts += mm_nt(src_hot, dst_hot)
        for side, (near, far) in enumerate(((src_mask, dst_hot), (dst_mask, src_hot))):
            chosen = hot(edge_id == neg_ref[0, 0, b, side : side + 1, :])
            negative = mm(far, chosen).astype(BF)
            times = mm_nt(ones, negative)[0:1, :]
            pairs += jnp.sum(near, axis=1, keepdims=True) * times
    return (pairs + pairs.T) * (1.0 / samples), counts + counts.T


def kernel(
    ndom, nrep,
    emb_hbm, sum_hbm, lists_hbm, src_hbm, dst_hbm, neg_hbm, rows_out, sum_out,
    emb_ref, sum_ref, lists_ref, src_ref, dst_ref, neg_ref,
    req_send, req_recv, pull_send, buf, grad_send, grad_recv, ids_all, halves,
    in_sem, req_ss, req_rs, pull_ss, pull_rs, ret_ss, ret_rs, rep_ss, rep_rs, ids_ss, ids_rs,
):
    me = lax.axis_index("dom")
    rep = lax.axis_index("rep")
    width, rows = emb_ref.shape
    capacity = lists_ref.shape[3]
    slots = ndom * capacity
    relay = nrep == 4

    def up(c):
        return lax.rem(me + c, ndom)

    def down(c):
        return lax.rem(me + ndom - c, ndom)

    def rep_peer(k):
        flipped = rep
        bit = 1
        while bit < nrep:
            if k & bit:
                flipped = flipped + bit - 2 * bit * lax.rem(rep // bit, 2)
            bit *= 2
        return flipped

    def size(c):
        return capacity if c < HEAVY else min(LIGHT_ROWS, capacity)

    barrier = pltpu.get_barrier_semaphore()
    for c in range(1, ndom):
        pl.semaphore_signal(barrier, inc=1, device_id={"dom": up(c)}, device_id_type=MESH)
    for k in range(1, nrep):
        pl.semaphore_signal(barrier, inc=1, device_id={"rep": rep_peer(k)}, device_id_type=MESH)

    loads = []
    for i, (hbm, ref) in enumerate((
        (lists_hbm, lists_ref), (src_hbm, src_ref), (dst_hbm, dst_ref), (neg_hbm, neg_ref), (emb_hbm, emb_ref), (sum_hbm, sum_ref)
    )):
        load = pltpu.make_async_copy(hbm, ref, in_sem.at[i])
        load.start()
        loads.append(load)

    for c in range(ndom):
        if size(c) < capacity:
            rest = capacity - size(c)
            buf[up(c), size(c) :, :] = jnp.zeros((rest, width), F32)
            for g in range(nrep):
                grad_recv[g, down(c), size(c) :, :] = jnp.zeros((rest, width), F32)

    loads[0].wait()
    own_lists = lists_ref[0, 0]
    if slots > capacity:
        own_lists = jnp.concatenate([own_lists, jnp.zeros((ndom, slots - capacity), jnp.int32)], axis=1)
    own_lists = pltpu.roll(own_lists, me * capacity, 1)
    for o in range(ndom):
        req_send[o] = own_lists[o : o + 1, :]

    pl.semaphore_wait(barrier, ndom - 1 + nrep - 1)

    def remote(src, dst, send, recv, target):
        return pltpu.make_async_remote_copy(
            src_ref=src, dst_ref=dst, send_sem=send, recv_sem=recv, device_id=target, device_id_type=MESH
        )

    asks = []
    for c in range(1, ndom):
        ask = remote(req_send.at[up(c)], req_recv.at[c], req_ss.at[c], req_rs.at[c], {"dom": up(c)})
        ask.start()
        asks.append(ask)

    for load in loads[1:]:
        load.wait()
    emb_parts = parts_of(emb_ref[...], 3)
    pairs, counts = pair_counts(src_ref, dst_ref, neg_ref, slots)

    ids = req_send[me]
    for c in range(1, ndom):
        asks[c - 1].wait_recv()
        ids = ids + req_recv[c]
    ids_all[rep] = ids

    row_id = lax.broadcasted_iota(jnp.int32, (slots, rows), 1)

    def hot_rows(row):
        return hot(row_id == jnp.broadcast_to(row, (8, slots)).T[:, 0:1])

    wanted = hot_rows(ids)
    pulled = mm_nt(wanted, emb_parts[0]) + mm_nt(wanted, emb_parts[1]) + mm_nt(wanted, emb_parts[2])
    pull_send[...] = pulled.reshape(ndom, capacity, width)
    pulls = []
    for c in range(1, ndom):
        live = pl.ds(0, size(c))
        pull = remote(
            pull_send.at[down(c), live], buf.at[me, live], pull_ss.at[c], pull_rs.at[c], {"dom": down(c)}
        )
        pull.start()
        pulls.append(pull)
    buf[me] = pull_send[me]
    tells = []
    for k in range(1, nrep):
        tell = remote(ids_all.at[rep], ids_all.at[rep], ids_ss.at[k], ids_rs.at[k], {"rep": rep_peer(k)})
        tell.start()
        tells.append(tell)

    for c in range(1, ndom):
        block = buf.at[up(c), pl.ds(0, size(c))]
        remote(block, block, pull_ss.at[c], pull_rs.at[c], {"dom": up(c)}).wait_recv()
    buffer = buf[...].reshape(slots, width)
    gram = lax.dot_general(buffer, buffer, (((1,), (1,)), ((), ())), precision=HI, preferred_element_type=F32)
    mixed = pairs * jax.nn.sigmoid(gram) - counts * jax.nn.sigmoid(-gram)
    gradient = jnp.dot(mixed, buffer, precision=HI, preferred_element_type=F32)
    grad_send[...] = gradient.reshape(ndom, capacity, width)

    returns = []
    for c in range(1, ndom):
        live = pl.ds(0, size(c))
        back = remote(
            grad_send.at[up(c), live], grad_recv.at[rep, me, live], ret_ss.at[c], ret_rs.at[c], {"dom": up(c)}
        )
        back.start()
        returns.append(back)
    grad_recv[rep, me] = grad_send[me]

    direct = [2, 1] if relay else list(range(1, nrep))

    def share(g, c, k, to):
        block = grad_recv.at[g, down(c), pl.ds(0, size(c))]
        return remote(block, block, rep_ss.at[k, c], rep_rs.at[k, c], {"rep": to})

    shares = []
    for c in range(ndom):
        if c > 0:
            block = grad_recv.at[rep, down(c), pl.ds(0, size(c))]
            remote(block, block, ret_ss.at[c], ret_rs.at[c], {"dom": down(c)}).wait_recv()
        for k in direct:
            sent = share(rep, c, k, rep_peer(k))
            sent.start()
            shares.append(sent)

    for tell in tells:
        tell.wait_recv()

    def arrived(k, c):
        share(rep_peer(k), c, k, rep_peer(k)).wait_recv()

    def half_sum(half, first):
        groups = max(nrep // 2, 1)
        total = jnp.zeros((width, rows), F32)
        hots = [hot_rows(ids_all[first + g]) for g in range(groups)]
        stacked = jnp.concatenate(hots, axis=0)
        data = grad_recv[pl.ds(first, groups)].reshape(groups * slots, width)
        for part in parts_of(data, 2):
            total += lax.dot_general(part, stacked, (((0,), (0,)), ((), ())), preferred_element_type=F32)
        halves[half] = total

    if relay:
        chip = rep // 2
        for c in range(ndom):
            arrived(1, c)
        half_sum(chip, 2 * chip)
        for c in range(ndom):
            arrived(2, c)
            sent = share(rep_peer(2), c, 3, rep_peer(1))
            sent.start()
            shares.append(sent)
        for c in range(ndom):
            arrived(3, c)
        half_sum(1 - chip, 2 - 2 * chip)
    else:
        for k in direct:
            for c in range(ndom):
                arrived(k, c)
        half_sum(0, 0)
        half_sum(1, nrep // 2)
    row_grad = halves[0] + halves[1]
    new_sum = sum_ref[...] + jnp.sum(row_grad * row_grad, axis=0, keepdims=True) * (1.0 / width)
    sum_out[...] = new_sum
    rows_out[...] = emb_ref[...] - row_grad * (learn_rate / jnp.sqrt(new_sum))

    for copy in asks + pulls + tells + returns + shares:
        copy.wait_send()


def local(ndom, nrep, embedding, adagrad_sum, row_lists, source_slots, target_slots, negative_ids):
    rows, width = embedding.shape
    capacity = row_lists.shape[3]
    slots = ndom * capacity
    dma = pltpu.SemaphoreType.DMA
    vmem = pl.BlockSpec(memory_space=pltpu.VMEM)
    new_rows, new_sum = pl.pallas_call(
        functools.partial(kernel, ndom, nrep),
        out_shape=(jax.ShapeDtypeStruct((width, rows), F32), jax.ShapeDtypeStruct((1, rows), F32)),
        in_specs=[pl.BlockSpec(memory_space=pl.ANY)] * 6,
        out_specs=(vmem, vmem),
        scratch_shapes=[
            pltpu.VMEM((width, rows), F32),
            pltpu.VMEM((1, rows), F32),
            pltpu.VMEM(row_lists.shape, jnp.int32),
            pltpu.VMEM(source_slots.shape, jnp.int32),
            pltpu.VMEM(target_slots.shape, jnp.int32),
            pltpu.VMEM(negative_ids.shape, jnp.int32),
            pltpu.VMEM((ndom, 1, slots), jnp.int32),
            pltpu.VMEM((ndom, 1, slots), jnp.int32),
            pltpu.VMEM((ndom, capacity, width), F32),
            pltpu.VMEM((ndom, capacity, width), F32),
            pltpu.VMEM((ndom, capacity, width), F32),
            pltpu.VMEM((nrep, ndom, capacity, width), F32),
            pltpu.VMEM((nrep, 1, slots), jnp.int32),
            pltpu.VMEM((2, width, rows), F32),
            dma((6,)),
            dma((ndom,)), dma((ndom,)), dma((ndom,)), dma((ndom,)), dma((ndom,)), dma((ndom,)),
            dma((nrep, ndom)), dma((nrep, ndom)), dma((nrep,)), dma((nrep,)),
        ],
        compiler_params=pltpu.CompilerParams(
            collective_id=0, has_side_effects=True, vmem_limit_bytes=60 * 1024 * 1024
        ),
    )(embedding.T, adagrad_sum.reshape(1, rows), row_lists, source_slots, target_slots, negative_ids)
    return (new_rows.T, new_sum.reshape(rows))


def solution(mesh):
    in_specs = (
        P("dom", None),
        P("dom"),
        P("rep", "dom", None, None),
        P("rep", "dom", None, None),
        P("rep", "dom", None, None),
        P("rep", "dom", None, None, None),
    )
    out_specs = (P("dom", None), P("dom"))
    body = functools.partial(local, mesh.shape["dom"], mesh.shape["rep"])
    return jax.shard_map(body, mesh=mesh, in_specs=in_specs, out_specs=out_specs, check_vma=False)
```

```python
import functools
import jax
import jax.numpy as jnp
from jax import lax
from jax.experimental import pallas as pl
from jax.experimental.pallas import tpu as pltpu
from jax.sharding import PartitionSpec as P

learn_rate = 0.1
HI = lax.Precision.HIGHEST
HEAVY = 4
LIGHT_ROWS = 8
MESH = pl.DeviceIdType.MESH
BF = jnp.bfloat16
F32 = jnp.float32


def mm(a, b):
    return lax.dot_general(a, b, (((1,), (0,)), ((), ())), preferred_element_type=F32)


def mm_nt(a, b):
    return lax.dot_general(a, b, (((1,), (1,)), ((), ())), preferred_element_type=F32)


def parts_of(x, count):
    parts = []
    for _ in range(count):
        part = x.astype(BF)
        parts.append(part)
        x = x - part.astype(F32)
    return parts


def hot(mask):
    return mask.astype(F32).astype(BF)


def pair_counts(src_ref, dst_ref, neg_ref, slots):
    batches, edges = src_ref.shape[2:]
    samples = neg_ref.shape[4]
    slot_id = lax.broadcasted_iota(jnp.int32, (slots, edges), 0)
    edge_id = lax.broadcasted_iota(jnp.int32, (edges, samples), 0)
    ones = jnp.ones((8, samples), BF)
    pairs = jnp.zeros((slots, slots), F32)
    counts = jnp.zeros((slots, slots), F32)
    for b in range(batches):
        src_mask = (slot_id == src_ref[0, 0, b : b + 1, :]).astype(F32)
        dst_mask = (slot_id == dst_ref[0, 0, b : b + 1, :]).astype(F32)
        src_hot = src_mask.astype(BF)
        dst_hot = dst_mask.astype(BF)
        counts += mm_nt(src_hot, dst_hot)
        for side, (near, far) in enumerate(((src_mask, dst_hot), (dst_mask, src_hot))):
            chosen = hot(edge_id == neg_ref[0, 0, b, side : side + 1, :])
            negative = mm(far, chosen).astype(BF)
            times = mm_nt(ones, negative)[0:1, :]
            pairs += jnp.sum(near, axis=1, keepdims=True) * times
    return (pairs + pairs.T) * (1.0 / samples), counts + counts.T


def kernel(
    ndom, nrep,
    emb_hbm, lists_hbm, src_hbm, dst_hbm, neg_hbm, total_out,
    emb_ref, lists_ref, src_ref, dst_ref, neg_ref,
    req_send, req_recv, pull_send, buf, grad_send, grad_recv, ids_all, halves,
    in_sem, req_ss, req_rs, pull_ss, pull_rs, ret_ss, ret_rs, rep_ss, rep_rs, ids_ss, ids_rs,
):
    me = lax.axis_index("dom")
    rep = lax.axis_index("rep")
    width, rows = emb_ref.shape
    capacity = lists_ref.shape[3]
    slots = ndom * capacity
    relay = nrep == 4

    def flip(index, count, k):
        flipped = index
        bit = 1
        while bit < count:
            if k & bit:
                flipped = flipped + bit - 2 * bit * lax.rem(index // bit, 2)
            bit *= 2
        return flipped

    paired = ndom & (ndom - 1) == 0

    def to(k):
        return flip(me, ndom, k) if paired else lax.rem(me + k, ndom)

    def source(k):
        return flip(me, ndom, k) if paired else lax.rem(me + ndom - k, ndom)

    def rep_peer(k):
        return flip(rep, nrep, k)

    light = min(LIGHT_ROWS, capacity)

    def units(owner, worker, act):
        act(0, pl.ds(0, light))
        if light < capacity:
            @pl.when(lax.rem(owner - worker + ndom, ndom) < HEAVY)
            def _():
                act(1, pl.ds(light, capacity - light))

    barrier = pltpu.get_barrier_semaphore()
    for c in range(1, ndom):
        pl.semaphore_signal(barrier, inc=1, device_id={"dom": to(c)}, device_id_type=MESH)
    for k in range(1, nrep):
        pl.semaphore_signal(barrier, inc=1, device_id={"rep": rep_peer(k)}, device_id_type=MESH)

    loads = []
    for i, (hbm, ref) in enumerate((
        (lists_hbm, lists_ref), (src_hbm, src_ref), (dst_hbm, dst_ref), (neg_hbm, neg_ref), (emb_hbm, emb_ref)
    )):
        load = pltpu.make_async_copy(hbm, ref, in_sem.at[i])
        load.start()
        loads.append(load)

    if light < capacity:
        for k in range(1, ndom):
            buf[source(k), light:, :] = jnp.zeros((capacity - light, width), F32)
            for g in range(nrep):
                @pl.when(lax.rem(me - source(k) + ndom, ndom) >= HEAVY)
                def _():
                    grad_recv[g, source(k), light:, :] = jnp.zeros((capacity - light, width), F32)

    loads[0].wait()
    own_lists = lists_ref[0, 0]
    if slots > capacity:
        own_lists = jnp.concatenate([own_lists, jnp.zeros((ndom, slots - capacity), jnp.int32)], axis=1)
    own_lists = pltpu.roll(own_lists, me * capacity, 1)
    for o in range(ndom):
        req_send[o] = own_lists[o : o + 1, :]

    pl.semaphore_wait(barrier, ndom - 1 + nrep - 1)

    def remote(src, dst, send, recv, target):
        return pltpu.make_async_remote_copy(
            src_ref=src, dst_ref=dst, send_sem=send, recv_sem=recv, device_id=target, device_id_type=MESH
        )

    asks = []
    for c in range(1, ndom):
        ask = remote(req_send.at[to(c)], req_recv.at[c], req_ss.at[c], req_rs.at[c], {"dom": to(c)})
        ask.start()
        asks.append(ask)

    for load in loads[1:]:
        load.wait()
    emb_parts = parts_of(emb_ref[...], 2)
    pairs, counts = pair_counts(src_ref, dst_ref, neg_ref, slots)

    ids = req_send[me]
    for c in range(1, ndom):
        asks[c - 1].wait_recv()
        ids = ids + req_recv[c]
    ids_all[rep] = ids

    row_id = lax.broadcasted_iota(jnp.int32, (slots, rows), 1)

    def hot_rows(row):
        return hot(row_id == jnp.broadcast_to(row, (8, slots)).T[:, 0:1])

    wanted = hot_rows(ids)
    pulled = mm_nt(wanted, emb_parts[0]) + mm_nt(wanted, emb_parts[1])
    pull_send[...] = pulled.reshape(ndom, capacity, width)
    def pull(k, worker):
        def copy(u, live):
            return remote(pull_send.at[worker, live], buf.at[me, live], pull_ss.at[k, u], pull_rs.at[k, u], {"dom": worker})
        return copy

    for k in range(1, ndom):
        units(me, to(k), lambda u, live: pull(k, to(k))(u, live).start())
    buf[me] = pull_send[me]
    tells = []
    for k in range(1, nrep):
        tell = remote(ids_all.at[rep], ids_all.at[rep], ids_ss.at[k], ids_rs.at[k], {"rep": rep_peer(k)})
        tell.start()
        tells.append(tell)

    for k in range(1, ndom):
        def landed(u, live):
            block = buf.at[source(k), live]
            remote(block, block, pull_ss.at[k, u], pull_rs.at[k, u], {"dom": source(k)}).wait_recv()
        units(source(k), me, landed)
    high, low = parts_of(buf[...].reshape(slots, width), 2)
    crossed = mm_nt(jnp.concatenate([high, low], axis=0), high)
    gram = crossed[:slots] + (crossed[slots:] + crossed[slots:].T)
    mixed = pairs * jax.nn.sigmoid(gram) - counts * jax.nn.sigmoid(-gram)
    mixed_high, mixed_low = parts_of(mixed, 2)
    gradient = mm(mixed_high, high) + (mm(mixed_high, low) + mm(mixed_low, high))
    grad_send[...] = gradient.reshape(ndom, capacity, width)

    def back(k, owner):
        def copy(u, live):
            return remote(grad_send.at[owner, live], grad_recv.at[rep, me, live], ret_ss.at[k, u], ret_rs.at[k, u], {"dom": owner})
        return copy

    for k in range(1, ndom):
        units(to(k), me, lambda u, live: back(k, to(k))(u, live).start())
    grad_recv[rep, me] = grad_send[me]

    direct = [2, 1] if relay else list(range(1, nrep))

    def share(g, k, p, peer):
        def copy(u, live):
            block = grad_recv.at[g, source(k), live]
            return remote(block, block, rep_ss.at[p, k, u], rep_rs.at[p, k, u], {"rep": peer})
        return copy

    for k in range(ndom):
        def pass_on(u, live):
            if k > 0:
                block = grad_recv.at[rep, source(k), live]
                remote(block, block, ret_ss.at[k, u], ret_rs.at[k, u], {"dom": source(k)}).wait_recv()
            for p in direct:
                share(rep, k, p, rep_peer(p))(u, live).start()
        units(me, source(k), pass_on)

    for tell in tells:
        tell.wait_recv()

    def arrived(p, k, then=None):
        def wait(u, live):
            share(rep_peer(p), k, p, rep_peer(p))(u, live).wait_recv()
            if then is not None:
                then(u, live)
        units(me, source(k), wait)

    def half_sum(half, first):
        groups = max(nrep // 2, 1)
        total = jnp.zeros((width, rows), F32)
        hots = [hot_rows(ids_all[first + g]) for g in range(groups)]
        stacked = jnp.concatenate(hots, axis=0)
        data = grad_recv[pl.ds(first, groups)].reshape(groups * slots, width)
        for part in parts_of(data, 2):
            total += lax.dot_general(part, stacked, (((0,), (0,)), ((), ())), preferred_element_type=F32)
        halves[half] = total

    if relay:
        chip = rep // 2
        for k in range(ndom):
            arrived(1, k)
        half_sum(chip, 2 * chip)
        for k in range(ndom):
            arrived(2, k, lambda u, live: share(rep_peer(2), k, 3, rep_peer(1))(u, live).start())
        for k in range(ndom):
            arrived(3, k)
        half_sum(1 - chip, 2 - 2 * chip)
    else:
        for p in direct:
            for k in range(ndom):
                arrived(p, k)
        half_sum(0, 0)
        half_sum(1, nrep // 2)
    total_out[...] = halves[0] + halves[1]

    for copy in asks + tells:
        copy.wait_send()
    for k in range(ndom):
        if k > 0:
            units(me, to(k), lambda u, live: pull(k, to(k))(u, live).wait_send())
            units(to(k), me, lambda u, live: back(k, to(k))(u, live).wait_send())
        for p in direct:
            units(me, source(k), lambda u, live: share(rep, k, p, rep_peer(p))(u, live).wait_send())
        if relay:
            units(me, source(k), lambda u, live: share(rep_peer(2), k, 3, rep_peer(1))(u, live).wait_send())


def adagrad(total_ref, emb_ref, sum_ref, rows_out, sum_out):
    row_grad = total_ref[...]
    width = row_grad.shape[0]
    new_sum = sum_ref[...] + jnp.sum(row_grad * row_grad, axis=0, keepdims=True) * (1.0 / width)
    sum_out[...] = new_sum
    rows_out[...] = emb_ref[...] - row_grad * (learn_rate / jnp.sqrt(new_sum))


def local(ndom, nrep, embedding, adagrad_sum, row_lists, source_slots, target_slots, negative_ids):
    rows, width = embedding.shape
    capacity = row_lists.shape[3]
    slots = ndom * capacity
    dma = pltpu.SemaphoreType.DMA
    vmem = pl.BlockSpec(memory_space=pltpu.VMEM)
    table = embedding.T
    total = pl.pallas_call(
        functools.partial(kernel, ndom, nrep),
        out_shape=jax.ShapeDtypeStruct((width, rows), F32),
        in_specs=[pl.BlockSpec(memory_space=pltpu.HBM)] * 5,
        out_specs=vmem,
        scratch_shapes=[
            pltpu.VMEM((width, rows), F32),
            pltpu.VMEM(row_lists.shape, jnp.int32),
            pltpu.VMEM(source_slots.shape, jnp.int32),
            pltpu.VMEM(target_slots.shape, jnp.int32),
            pltpu.VMEM(negative_ids.shape, jnp.int32),
            pltpu.VMEM((ndom, 1, slots), jnp.int32),
            pltpu.VMEM((ndom, 1, slots), jnp.int32),
            pltpu.VMEM((ndom, capacity, width), F32),
            pltpu.VMEM((ndom, capacity, width), F32),
            pltpu.VMEM((ndom, capacity, width), F32),
            pltpu.VMEM((nrep, ndom, capacity, width), F32),
            pltpu.VMEM((nrep, 1, slots), jnp.int32),
            pltpu.VMEM((2, width, rows), F32),
            dma((5,)),
            dma((ndom,)), dma((ndom,)), dma((ndom, 2)), dma((ndom, 2)), dma((ndom, 2)), dma((ndom, 2)),
            dma((nrep, ndom, 2)), dma((nrep, ndom, 2)), dma((nrep,)), dma((nrep,)),
        ],
        compiler_params=pltpu.CompilerParams(
            collective_id=0, has_side_effects=True, vmem_limit_bytes=60 << 20
        ),
    )(table, row_lists, source_slots, target_slots, negative_ids)
    steps = 2 if rows % 256 == 0 else 1
    block = pl.BlockSpec((width, rows // steps), lambda i: (0, i))
    line = pl.BlockSpec((1, rows // steps), lambda i: (0, i))
    new_rows, new_sum = pl.pallas_call(
        adagrad,
        out_shape=(jax.ShapeDtypeStruct((width, rows), F32), jax.ShapeDtypeStruct((1, rows), F32)),
        grid=(steps,),
        in_specs=[block, block, line],
        out_specs=(block, line),
        compiler_params=pltpu.CompilerParams(vmem_limit_bytes=60 << 20),
    )(total, table, adagrad_sum.reshape(1, rows))
    return (new_rows.T, new_sum.reshape(rows))


def solution(mesh):
    in_specs = (
        P("dom", None),
        P("dom"),
        P("rep", "dom", None, None),
        P("rep", "dom", None, None),
        P("rep", "dom", None, None),
        P("rep", "dom", None, None, None),
    )
    out_specs = (P("dom", None), P("dom"))
    body = functools.partial(local, mesh.shape["dom"], mesh.shape["rep"])
    return jax.shard_map(body, mesh=mesh, in_specs=in_specs, out_specs=out_specs, check_vma=False)
```

```python
import functools
import jax
import jax.numpy as jnp
from jax import lax
from jax.experimental import pallas as pl
from jax.experimental.pallas import tpu as pltpu
from jax.sharding import PartitionSpec as P

learn_rate = 0.1
HI = lax.Precision.HIGHEST
HEAVY = 4
LIGHT_ROWS = 8
MESH = pl.DeviceIdType.MESH
BF = jnp.bfloat16
F32 = jnp.float32


def mm(a, b):
    return lax.dot_general(a, b, (((1,), (0,)), ((), ())), preferred_element_type=F32)


def mm_nt(a, b):
    return lax.dot_general(a, b, (((1,), (1,)), ((), ())), preferred_element_type=F32)


def parts_of(x, count):
    parts = []
    for _ in range(count):
        part = x.astype(BF)
        parts.append(part)
        x = x - part.astype(F32)
    return parts


def hot(mask):
    return mask.astype(F32).astype(BF)


def pair_counts(batches, src_ref, dst_ref, neg_ref, slots):
    edges = src_ref.shape[3]
    samples = neg_ref.shape[4]
    groups = -(-edges // 128)
    slot_id = lax.broadcasted_iota(jnp.int32, (slots, edges), 0)
    lane_id = lax.broadcasted_iota(jnp.int32, (128, samples), 0)
    group_id = lax.broadcasted_iota(jnp.int32, (-(-groups // 8) * 8, samples), 0)
    pairs = jnp.zeros((slots, slots), F32)
    counts = jnp.zeros((slots, slots), F32)
    for b in batches:
        src_mask = (slot_id == src_ref[0, 0, b : b + 1, :]).astype(F32)
        dst_mask = (slot_id == dst_ref[0, 0, b : b + 1, :]).astype(F32)
        src_hot = src_mask.astype(BF)
        dst_hot = dst_mask.astype(BF)
        counts += mm_nt(src_hot, dst_hot)
        for side, (near, far) in enumerate(((src_mask, dst_hot), (dst_mask, src_hot))):
            drawn = neg_ref[0, 0, b, side : side + 1, :]
            in_lane = hot(lane_id == jnp.bitwise_and(drawn, 127))
            in_group = hot(group_id == lax.shift_right_logical(drawn, jnp.full_like(drawn, 7)))
            table = mm_nt(in_group, in_lane)
            drawn_times = jnp.concatenate([table[g : g + 1] for g in range(groups)], axis=1)[:, :edges]
            drawn_high, drawn_low = parts_of(jnp.broadcast_to(drawn_times, (8, edges)), 2)
            times = (mm_nt(drawn_high, far) + mm_nt(drawn_low, far))[0:1, :]
            pairs += jnp.sum(near, axis=1, keepdims=True) * times
    return pairs, counts


def kernel(
    ndom, nrep,
    emb_hbm, lists_hbm, src_hbm, dst_hbm, neg_hbm, total_out,
    emb_ref, lists_ref, src_ref, dst_ref, neg_ref,
    req_send, req_recv, pull_send, buf, grad_send, grad_recv, ids_all, halves,
    in_sem, req_ss, req_rs, pull_ss, pull_rs, ret_ss, ret_rs, rep_ss, rep_rs, ids_ss, ids_rs,
):
    me = lax.axis_index("dom")
    rep = lax.axis_index("rep")
    width, rows = emb_ref.shape
    capacity = lists_ref.shape[3]
    slots = ndom * capacity
    relay = nrep == 4

    def flip(index, count, k):
        flipped = index
        bit = 1
        while bit < count:
            if k & bit:
                flipped = flipped + bit - 2 * bit * lax.rem(index // bit, 2)
            bit *= 2
        return flipped

    paired = ndom & (ndom - 1) == 0

    def to(k):
        return flip(me, ndom, k) if paired else lax.rem(me + k, ndom)

    def source(k):
        return flip(me, ndom, k) if paired else lax.rem(me + ndom - k, ndom)

    def rep_peer(k):
        return flip(rep, nrep, k)

    light = min(LIGHT_ROWS, capacity)

    def units(owner, worker, act):
        act(0, pl.ds(0, light))
        if light < capacity:
            @pl.when(lax.rem(owner - worker + ndom, ndom) < HEAVY)
            def _():
                act(1, pl.ds(light, capacity - light))

    barrier = pltpu.get_barrier_semaphore()
    for c in range(1, ndom):
        pl.semaphore_signal(barrier, inc=1, device_id={"dom": to(c)}, device_id_type=MESH)
    for k in range(1, nrep):
        pl.semaphore_signal(barrier, inc=1, device_id={"rep": rep_peer(k)}, device_id_type=MESH)

    loads = []
    for i, (hbm, ref) in enumerate((
        (lists_hbm, lists_ref), (src_hbm, src_ref), (dst_hbm, dst_ref), (neg_hbm, neg_ref), (emb_hbm, emb_ref)
    )):
        load = pltpu.make_async_copy(hbm, ref, in_sem.at[i])
        load.start()
        loads.append(load)

    if light < capacity:
        for k in range(1, ndom):
            buf[source(k), light:, :] = jnp.zeros((capacity - light, width), F32)
            for g in range(nrep):
                @pl.when(lax.rem(me - source(k) + ndom, ndom) >= HEAVY)
                def _():
                    grad_recv[g, source(k), light:, :] = jnp.zeros((capacity - light, width), F32)

    loads[0].wait()
    own_lists = lists_ref[0, 0]
    if slots > capacity:
        own_lists = jnp.concatenate([own_lists, jnp.zeros((ndom, slots - capacity), jnp.int32)], axis=1)
    own_lists = pltpu.roll(own_lists, me * capacity, 1)
    for o in range(ndom):
        req_send[o] = own_lists[o : o + 1, :]

    pl.semaphore_wait(barrier, ndom - 1 + nrep - 1)

    def remote(src, dst, send, recv, target):
        return pltpu.make_async_remote_copy(
            src_ref=src, dst_ref=dst, send_sem=send, recv_sem=recv, device_id=target, device_id_type=MESH
        )

    asks = []
    for c in range(1, ndom):
        ask = remote(req_send.at[to(c)], req_recv.at[c], req_ss.at[c], req_rs.at[c], {"dom": to(c)})
        ask.start()
        asks.append(ask)

    for load in loads[1:]:
        load.wait()
    emb_parts = parts_of(emb_ref[...], 2)
    batches = range(src_ref.shape[2])
    pairs, counts = pair_counts(batches[:1], src_ref, dst_ref, neg_ref, slots)

    ids = req_send[me]
    for c in range(1, ndom):
        asks[c - 1].wait_recv()
        ids = ids + req_recv[c]
    ids_all[rep] = ids

    row_id = lax.broadcasted_iota(jnp.int32, (slots, rows), 1)

    def hot_rows(row):
        return hot(row_id == jnp.broadcast_to(row, (8, slots)).T[:, 0:1])

    wanted = hot_rows(ids)
    pulled = mm_nt(wanted, emb_parts[0]) + mm_nt(wanted, emb_parts[1])
    pull_send[...] = pulled.reshape(ndom, capacity, width)
    def pull(k, worker):
        def copy(u, live):
            return remote(pull_send.at[worker, live], buf.at[me, live], pull_ss.at[k, u], pull_rs.at[k, u], {"dom": worker})
        return copy

    for k in range(1, ndom):
        units(me, to(k), lambda u, live: pull(k, to(k))(u, live).start())
    buf[me] = pull_send[me]
    tells = []
    for k in range(1, nrep):
        tell = remote(ids_all.at[rep], ids_all.at[rep], ids_ss.at[k], ids_rs.at[k], {"rep": rep_peer(k)})
        tell.start()
        tells.append(tell)

    more_pairs, more_counts = pair_counts(batches[1:], src_ref, dst_ref, neg_ref, slots)
    pairs, counts = pairs + more_pairs, counts + more_counts
    pairs = (pairs + pairs.T) * (1.0 / neg_ref.shape[4])
    counts = counts + counts.T

    for k in range(1, ndom):
        def landed(u, live):
            block = buf.at[source(k), live]
            remote(block, block, pull_ss.at[k, u], pull_rs.at[k, u], {"dom": source(k)}).wait_recv()
        units(source(k), me, landed)
    high, low = parts_of(buf[...].reshape(slots, width), 2)
    crossed = mm_nt(jnp.concatenate([high, low], axis=0), high)
    gram = crossed[:slots] + (crossed[slots:] + crossed[slots:].T)
    mixed = pairs * jax.nn.sigmoid(gram) - counts * jax.nn.sigmoid(-gram)
    mixed_high, mixed_low = parts_of(mixed, 2)
    gradient = mm(mixed_high, high) + (mm(mixed_high, low) + mm(mixed_low, high))
    grad_send[...] = gradient.reshape(ndom, capacity, width)

    def back(k, owner):
        def copy(u, live):
            return remote(grad_send.at[owner, live], grad_recv.at[rep, me, live], ret_ss.at[k, u], ret_rs.at[k, u], {"dom": owner})
        return copy

    for k in range(1, ndom):
        units(to(k), me, lambda u, live: back(k, to(k))(u, live).start())
    grad_recv[rep, me] = grad_send[me]

    for tell in tells:
        tell.wait_recv()
    groups = max(nrep // 2, 1)
    near_half = rep // 2 if relay else 0
    far_half = 1 - near_half
    owned = [
        jnp.concatenate([hot_rows(ids_all[groups * half + g]) for g in range(groups)], axis=0)
        for half in (near_half, far_half)
    ]

    direct = [2, 1] if relay else list(range(1, nrep))

    def share(g, k, p, peer):
        def copy(u, live):
            block = grad_recv.at[g, source(k), live]
            return remote(block, block, rep_ss.at[p, k, u], rep_rs.at[p, k, u], {"rep": peer})
        return copy

    for k in range(ndom):
        def pass_on(u, live):
            if k > 0:
                block = grad_recv.at[rep, source(k), live]
                remote(block, block, ret_ss.at[k, u], ret_rs.at[k, u], {"dom": source(k)}).wait_recv()
            for p in direct:
                share(rep, k, p, rep_peer(p))(u, live).start()
        units(me, source(k), pass_on)


    def arrived(p, k, then=None):
        def wait(u, live):
            share(rep_peer(p), k, p, rep_peer(p))(u, live).wait_recv()
            if then is not None:
                then(u, live)
        units(me, source(k), wait)

    def half_sum(half, stacked):
        total = jnp.zeros((width, rows), F32)
        data = grad_recv[pl.ds(groups * half, groups)].reshape(groups * slots, width)
        for part in parts_of(data, 2):
            total += lax.dot_general(part, stacked, (((0,), (0,)), ((), ())), preferred_element_type=F32)
        halves[half] = total

    if relay:
        for k in range(ndom):
            arrived(1, k)
        half_sum(near_half, owned[0])
        for k in range(ndom):
            arrived(2, k, lambda u, live: share(rep_peer(2), k, 3, rep_peer(1))(u, live).start())
        for k in range(ndom):
            arrived(3, k)
        half_sum(far_half, owned[1])
    else:
        for p in direct:
            for k in range(ndom):
                arrived(p, k)
        half_sum(near_half, owned[0])
        half_sum(far_half, owned[1])
    total_out[...] = halves[0] + halves[1]

    for copy in asks + tells:
        copy.wait_send()
    for k in range(ndom):
        if k > 0:
            units(me, to(k), lambda u, live: pull(k, to(k))(u, live).wait_send())
            units(to(k), me, lambda u, live: back(k, to(k))(u, live).wait_send())
        for p in direct:
            units(me, source(k), lambda u, live: share(rep, k, p, rep_peer(p))(u, live).wait_send())
        if relay:
            units(me, source(k), lambda u, live: share(rep_peer(2), k, 3, rep_peer(1))(u, live).wait_send())


def adagrad(total_ref, emb_ref, sum_ref, rows_out, sum_out):
    row_grad = total_ref[...]
    width = row_grad.shape[0]
    new_sum = sum_ref[...] + jnp.sum(row_grad * row_grad, axis=0, keepdims=True) * (1.0 / width)
    sum_out[...] = new_sum
    rows_out[...] = emb_ref[...] - row_grad * (learn_rate / jnp.sqrt(new_sum))


def local(ndom, nrep, embedding, adagrad_sum, row_lists, source_slots, target_slots, negative_ids):
    rows, width = embedding.shape
    capacity = row_lists.shape[3]
    slots = ndom * capacity
    dma = pltpu.SemaphoreType.DMA
    vmem = pl.BlockSpec(memory_space=pltpu.VMEM)
    table = embedding.T
    total = pl.pallas_call(
        functools.partial(kernel, ndom, nrep),
        out_shape=jax.ShapeDtypeStruct((width, rows), F32),
        in_specs=[pl.BlockSpec(memory_space=pltpu.HBM)] * 5,
        out_specs=vmem,
        scratch_shapes=[
            pltpu.VMEM((width, rows), F32),
            pltpu.VMEM(row_lists.shape, jnp.int32),
            pltpu.VMEM(source_slots.shape, jnp.int32),
            pltpu.VMEM(target_slots.shape, jnp.int32),
            pltpu.VMEM(negative_ids.shape, jnp.int32),
            pltpu.VMEM((ndom, 1, slots), jnp.int32),
            pltpu.VMEM((ndom, 1, slots), jnp.int32),
            pltpu.VMEM((ndom, capacity, width), F32),
            pltpu.VMEM((ndom, capacity, width), F32),
            pltpu.VMEM((ndom, capacity, width), F32),
            pltpu.VMEM((nrep, ndom, capacity, width), F32),
            pltpu.VMEM((nrep, 1, slots), jnp.int32),
            pltpu.VMEM((2, width, rows), F32),
            dma((5,)),
            dma((ndom,)), dma((ndom,)), dma((ndom, 2)), dma((ndom, 2)), dma((ndom, 2)), dma((ndom, 2)),
            dma((nrep, ndom, 2)), dma((nrep, ndom, 2)), dma((nrep,)), dma((nrep,)),
        ],
        compiler_params=pltpu.CompilerParams(
            collective_id=0, has_side_effects=True, vmem_limit_bytes=60 << 20
        ),
    )(table, row_lists, source_slots, target_slots, negative_ids)
    steps = 2 if rows % 256 == 0 else 1
    block = pl.BlockSpec((width, rows // steps), lambda i: (0, i))
    line = pl.BlockSpec((1, rows // steps), lambda i: (0, i))
    new_rows, new_sum = pl.pallas_call(
        adagrad,
        out_shape=(jax.ShapeDtypeStruct((width, rows), F32), jax.ShapeDtypeStruct((1, rows), F32)),
        grid=(steps,),
        in_specs=[block, block, line],
        out_specs=(block, line),
        compiler_params=pltpu.CompilerParams(vmem_limit_bytes=60 << 20),
    )(total, table, adagrad_sum.reshape(1, rows))
    return (new_rows.T, new_sum.reshape(rows))


def solution(mesh):
    in_specs = (
        P("dom", None),
        P("dom"),
        P("rep", "dom", None, None),
        P("rep", "dom", None, None),
        P("rep", "dom", None, None),
        P("rep", "dom", None, None, None),
    )
    out_specs = (P("dom", None), P("dom"))
    body = functools.partial(local, mesh.shape["dom"], mesh.shape["rep"])
    return jax.shard_map(body, mesh=mesh, in_specs=in_specs, out_specs=out_specs, check_vma=False)
```
